768 devices in a mesh: wave: 24 (over z, core), lev: 32 (over y, x).
Axes of the slice: x: 4, y: 8, z: 12, core: 2. Of those that a mesh axis runs over, the one named last changes fastest.
Arguments:
- spectral: bfloat16 [1296, 2, 3, 32, 1296], P('wave', None, None, 'lev'), may hold values from -6 to 6
- legendre: bfloat16 [1296, 24, 1296], P('wave'), may hold values from -0.15625 to 0.15625
- gauss: float32 [48], replicated, may hold values from 0.2 to 2
- wave_order: int32 [1296], replicated, may hold values from 0 to 1295, each once
- pair_order: int32 [24], replicated, may hold values from 0 to 23, each once
- nlon: int32 [24], replicated, may hold values from 4 to 4096, as said below
Outputs:
- grid: float32 [48, 3, 32, 4096], P('wave', None, None, 'lev')
- tendency: bfloat16 [1296, 2, 3, 32, 1296], P('wave', None, None, 'lev')
The draws below stay inside these ranges and needn't reach their ends.
Inputs may be any that keep to these rules, and one draw needn't show every extreme that they name: `wave_order`: each wavenumber is held by exactly one row. `pair_order`: each latitude pair is held by exactly one pair row. `nlon`: every count is a multiple of 4, and some pair has exactly 4096 points.
All inputs are finite; a program needn't handle non-finite values.
Results may differ from the reference program's by a relative error of at most 0.0074.
Values may be sent and summed in bfloat16 or wider, within the bound.
A program may use at most 128 MiB of HBM per device.

```python
import math
import jax
import jax.numpy as jnp
from jax import lax

FIELDS = 3
MW = 1296
NPAIR = 24
NLAT = 48
ATMOSPHERE_LAYER = 32
MERIDIAN_SLOTS = 4096


def draw_nlon(key, part):
    first_key, second_key = jax.random.split(key)
    counts = 4 * jax.random.randint(first_key, (NPAIR,), 1, MERIDIAN_SLOTS // 4 + 1)
    widest = jax.random.randint(second_key, (), 0, NPAIR)
    return jnp.where(lax.iota(jnp.int32, NPAIR) == widest, MERIDIAN_SLOTS, counts).astype(jnp.int32)


def shard_levels(key, extent, cuts, smallest, top_value):
    def one(position, blocks):
        draws = jax.random.uniform(jax.random.fold_in(jax.random.fold_in(key, 6), position), (blocks,), jnp.float32, smallest / len(cuts), top_value / len(cuts))
        return jnp.repeat(jnp.exp(draws), extent[position] // blocks).reshape((-1,) + (1,) * (len(extent) - position - 1))

    gain = one(*cuts[0])
    for cut in cuts[1:]:
        gain = gain * one(*cut)
    return gain


def scatter_about(own_key, shape, scale, most, cuts=(), dtype=jnp.bfloat16):
    factor_of = shard_levels(own_key, shape, cuts, -0.22, 0.18) if cuts else 1.0
    entries = jax.random.normal(own_key, shape, jnp.float32) * scale * factor_of
    return jnp.minimum(jnp.maximum(entries, -most), most).astype(dtype)


def setup_inputs(seed: int = 0) -> dict:
    key_of = jax.random.split(jax.random.key(seed), 7)
    spectral = scatter_about(key_of[0], (MW, 2, FIELDS, ATMOSPHERE_LAYER, MW), 1.0, 6.0, ((0, 24), (3, 32)))
    legendre = scatter_about(key_of[1], (MW, NPAIR, MW), MW ** -0.5, 0.15625, ((0, 24),))
    gauss = jnp.clip(jax.random.uniform(key_of[2], (NLAT,), jnp.float32, 0.2, 2.0), 0.2, 2.0)
    wave_order = jax.random.permutation(key_of[3], MW).astype(jnp.int32)
    pair_order = jax.random.permutation(key_of[4], NPAIR).astype(jnp.int32)
    nlon = draw_nlon(jax.random.fold_in(key_of[6], 71), 0)
    return {"spectral": spectral, "legendre": legendre, "gauss": gauss, "wave_order": wave_order, "pair_order": pair_order, "nlon": nlon}


def trig_tables(wavenumbers, points, offset, width):
    longitude = offset + lax.iota(jnp.int32, width)
    phases = wavenumbers[:, None] * longitude[None, :] % points
    angles = phases.astype(jnp.float32) * (2.0 * math.pi) / points.astype(jnp.float32)
    keep_mask = jnp.logical_and(2 * wavenumbers[:, None] < points, longitude[None, :] < points).astype(jnp.float32)
    return ((jnp.cos(angles) * keep_mask).astype(jnp.bfloat16), (jnp.sin(angles) * keep_mask).astype(jnp.bfloat16))

def reference(spectral, legendre, gauss, wave_order, pair_order, nlon):
    columns = 2 * FIELDS * ATMOSPHERE_LAYER
    midpoint_index = FIELDS * ATMOSPHERE_LAYER
    degree = lax.iota(jnp.int32, MW)
    maximal_degree_cutoff = lax.Precision.HIGHEST

    def forward_row(members):
        spectral_rows, legendre_rows, wavenumber = members
        flattened = spectral_rows.reshape(columns, MW).astype(jnp.float32)
        keep_mask = (degree >= wavenumber).astype(jnp.float32)
        parity = jnp.where((degree + wavenumber) % 2 == 0, 1.0, -1.0).astype(jnp.float32)
        matrix = legendre_rows.astype(jnp.float32).T
        northern = jnp.dot(flattened * keep_mask, matrix, precision=maximal_degree_cutoff)
        southern = jnp.dot(flattened * (keep_mask * parity), matrix, precision=maximal_degree_cutoff)
        return jnp.stack([northern, southern], axis=2).reshape(columns, NLAT)
    fourier = lax.map(forward_row, (spectral, legendre, wave_order)).astype(jnp.bfloat16)

    def per_latitude(latitude):
        points = nlon[latitude // 2]
        cosine, sine_part = trig_tables(wave_order, points, jnp.int32(0), MERIDIAN_SLOTS)
        broad_cos_table = cosine.astype(jnp.float32)
        broad_sin_table = sine_part.astype(jnp.float32)
        column = lax.dynamic_index_in_dim(fourier, latitude, 2, keepdims=False).astype(jnp.float32)
        real_part = column[:, :midpoint_index]
        imag_part = column[:, midpoint_index:]
        variable_bundle = (jnp.dot(real_part.T, broad_cos_table, precision=maximal_degree_cutoff) - jnp.dot(imag_part.T, broad_sin_table, precision=maximal_degree_cutoff)) * (1.0 / math.sqrt(MW))
        variable_bundle = variable_bundle.reshape(FIELDS, ATMOSPHERE_LAYER, MERIDIAN_SLOTS)
        latitudinal_flow = variable_bundle[0]
        poleward_flow = variable_bundle[1]
        heat_condition = variable_bundle[2]
        ground_barometric_datum = jnp.flip(jnp.cumsum(jnp.flip(heat_condition, 0), 0), 0) * (1.0 / math.sqrt(ATMOSPHERE_LAYER))
        scaled_summands = jnp.stack([latitudinal_flow * heat_condition, poleward_flow * heat_condition, latitudinal_flow * poleward_flow + ground_barometric_datum])
        scaled_summands = lax.optimization_barrier(scaled_summands.astype(jnp.bfloat16)).astype(jnp.float32).reshape(midpoint_index, MERIDIAN_SLOTS)
        weight_scale = gauss[latitude] / jnp.sqrt(points.astype(jnp.float32))
        recovered_realpart = jnp.dot(scaled_summands, broad_cos_table.T, precision=maximal_degree_cutoff)
        recovered_imaginary = -jnp.dot(scaled_summands, broad_sin_table.T, precision=maximal_degree_cutoff)
        weighted = (jnp.concatenate([recovered_realpart, recovered_imaginary], axis=0) * weight_scale).astype(jnp.bfloat16)
        return (variable_bundle, weighted)
    fields_all, weighted_all = lax.map(per_latitude, lax.iota(jnp.int32, NLAT))
    row_latitude = (2 * pair_order[:, None] + lax.iota(jnp.int32, 2)[None, :]).reshape(NLAT)
    grid = jnp.take(fields_all, row_latitude, axis=0)

    def backward_row(members):
        legendre_rows, wavenumber, row_index = members
        keep_mask = (degree >= wavenumber).astype(jnp.float32)
        parity = jnp.where((degree + wavenumber) % 2 == 0, 1.0, -1.0).astype(jnp.float32)
        latitude_block = lax.dynamic_index_in_dim(weighted_all, row_index, 2, keepdims=False).astype(jnp.float32)
        matrix = legendre_rows.astype(jnp.float32)
        both_halves = jnp.stack([matrix, matrix * parity[None, :]], axis=1).reshape(NLAT, MW)
        combined = jnp.dot(latitude_block.T, both_halves, precision=maximal_degree_cutoff) * keep_mask * math.sqrt(MW / NLAT)
        return combined.astype(jnp.bfloat16)
    tendency = lax.map(backward_row, (legendre, wave_order, lax.iota(jnp.int32, MW)))
    return (grid, tendency.reshape(MW, 2, FIELDS, ATMOSPHERE_LAYER, MW))
```

```python
import math

import jax
import jax.numpy as jnp
from jax import lax
from jax.sharding import PartitionSpec as P


def unit_circle(longitude, wavenumbers, points):
    product = longitude[:, None] * wavenumbers[None, :]
    turns = jnp.round(product / points)
    angles = (product - turns * points) * (2.0 * math.pi / points)
    return jnp.cos(angles), jnp.sin(angles)


def two_terms(x):
    high = x.astype(jnp.bfloat16)
    low = (x - high.astype(jnp.float32)).astype(jnp.bfloat16)
    return high, low


def local(spectral, legendre, gauss, wave_order, pair_order, nlon):
    rows, _, fields, _, modes = spectral.shape
    pairs = legendre.shape[1]
    levels = lax.axis_size("lev")
    wave_me = lax.axis_index("wave")
    lev_me = lax.axis_index("lev")
    columns = 2 * fields
    seg = 128
    bf16 = jnp.bfloat16
    f32 = jnp.float32
    highest = lax.Precision.HIGHEST
    own_modes = lax.dynamic_slice_in_dim(wave_order, wave_me * rows, rows)
    degree = lax.iota(jnp.int32, modes)
    upper = degree[None, :] >= own_modes[:, None]
    even = (degree[None, :] + own_modes[:, None]) % 2 == 0
    keep_north = upper.astype(bf16)
    keep_south = jnp.where(upper, jnp.where(even, 1.0, -1.0), 0.0).astype(bf16)
    flat = spectral.reshape(rows, columns, modes)
    both = jnp.concatenate([flat * keep_north[:, None, :], flat * keep_south[:, None, :]], axis=1)
    folded = jnp.einsum("ojb,oub->ujo", both, legendre, preferred_element_type=f32)
    pair_ids = lax.iota(jnp.int32, pairs)
    picker = (pair_order[:, None] == pair_ids[None, :]).astype(bf16)
    ordered = jnp.einsum(
        "ip,pcr->icr", picker, folded.astype(bf16), preferred_element_type=f32
    ).astype(bf16)
    received = lax.all_to_all(ordered, "wave", split_axis=0, concat_axis=2, tiled=True)
    coefficients = received.reshape(2, 2, fields, modes).astype(f32)
    my_pair = lax.dynamic_index_in_dim(pair_order, wave_me, 0, keepdims=False)
    points_int = jnp.sum(jnp.where(pair_ids == my_pair, nlon, 0))
    points = points_int.astype(f32)
    my_gauss = lax.dynamic_slice_in_dim(gauss, 2 * my_pair, 2)
    orders = wave_order.astype(f32)
    near_cos, near_sin = unit_circle(lax.iota(f32, seg), orders, points)
    far_cos, far_sin = unit_circle(lax.iota(f32, levels) * float(seg), orders, points)
    inside = (2 * wave_order < points_int).astype(f32)
    real = (coefficients[:, 0] * inside)[:, :, None, :]
    imag = (coefficients[:, 1] * inside)[:, :, None, :]
    turned_real = real * near_cos - imag * near_sin
    turned_imag = real * near_sin + imag * near_cos
    turned = jnp.stack([turned_real, turned_imag], axis=0).astype(bf16)
    far = jnp.stack([far_cos, -far_sin], axis=1)
    high, low = two_terms(far)
    far_terms = jnp.concatenate([high, low], axis=0)
    sums = jnp.einsum("acm,chfbm->ahfb", far_terms, turned, preferred_element_type=f32)
    sums = sums[:levels] + sums[levels:]
    longitude = (
        seg * lax.iota(jnp.int32, levels)[:, None] + lax.iota(jnp.int32, seg)[None, :]
    )
    scale = jnp.where(longitude < points_int, 1.0 / math.sqrt(modes), 0.0)
    by_segment = sums * scale[:, None, None, :]
    by_level = lax.all_to_all(by_segment, "lev", split_axis=0, concat_axis=0, tiled=True)
    pieces = jnp.moveaxis(by_level, 0, 2)
    east = pieces[:, 0]
    north = pieces[:, 1]
    heat = pieces[:, 2]
    level_ids = lax.iota(jnp.int32, levels)
    above = (level_ids[None, :] >= level_ids[:, None]).astype(f32)
    geopotential = jnp.einsum("el,slo->seo", above, heat, precision=highest) * (
        1.0 / math.sqrt(levels)
    )
    fluxes = jnp.stack(
        [east * heat, north * heat, east * north + geopotential], axis=1
    ).astype(bf16)
    back = lax.all_to_all(fluxes, "lev", split_axis=2, concat_axis=2, tiled=True)
    inner = jnp.einsum("hfab,acm->chfbm", back, far.astype(bf16), preferred_element_type=f32)
    inner_low = jnp.einsum("hfab,acm->chfbm", back, low, preferred_element_type=f32)
    inner = inner + inner_low
    gathered_cos = inner[0]
    gathered_sin = -inner[1]
    sum_real = jnp.sum(gathered_cos * near_cos - gathered_sin * near_sin, axis=2)
    sum_imag = -jnp.sum(gathered_cos * near_sin + gathered_sin * near_cos, axis=2)
    factor = (my_gauss / jnp.sqrt(points))[:, None, None, None] * inside
    weighted = (jnp.stack([sum_real, sum_imag], axis=1) * factor).astype(bf16)
    weighted = weighted.reshape(2 * columns, modes)
    returned = lax.all_to_all(
        weighted.reshape(1, 2 * columns, modes), "wave", split_axis=2, concat_axis=0, tiled=True
    )
    natural = jnp.einsum("ip,icr->rcp", picker, returned, preferred_element_type=f32).astype(bf16)
    contracted = jnp.einsum("rcp,rpn->rcn", natural, legendre, preferred_element_type=f32)
    parity = jnp.where(even, 1.0, -1.0).astype(f32)
    outer_scale = upper.astype(f32) * math.sqrt(modes / (2 * pairs))
    combined = (
        contracted[:, :columns] + parity[:, None, :] * contracted[:, columns:]
    ) * outer_scale[:, None, :]
    tendency = combined.astype(bf16).reshape(rows, 2, fields, 1, modes)
    return (pieces, tendency)


def solution(mesh):
    in_specs = (P("wave", None, None, "lev", None), P("wave", None, None), P(), P(), P(), P())
    out_specs = (P("wave", None, None, "lev"), P("wave", None, None, "lev", None))
    return jax.shard_map(local, mesh=mesh, in_specs=in_specs, out_specs=out_specs, check_vma=False)
```

```python
import functools
import math

import jax
import jax.numpy as jnp
from jax import lax
from jax.experimental import pallas as pl
from jax.experimental.pallas import tpu as pltpu
from jax.sharding import PartitionSpec as P

BF16 = jnp.bfloat16
F32 = jnp.float32
MESH = pl.DeviceIdType.MESH
SEG = 128
HALF = 64
ROWS_AT_ONCE = 3
SERIES = [(-1.0) ** i * (2.0 * math.pi) ** (2 * i + 1) / math.factorial(2 * i + 1) for i in range(6)]


def sine_of_turns(t):
    square = t * t
    total = jnp.full_like(t, SERIES[-1])
    for factor in SERIES[-2::-1]:
        total = total * square + factor
    return total * t


def unit_circle(product, points, inverse):
    t = (product - jnp.floor(product * inverse + 0.5) * points) * inverse
    folded = jnp.where(t > 0.25, 0.5 - t, jnp.where(t < -0.25, -0.5 - t, t))
    return sine_of_turns(0.25 - jnp.abs(t)), sine_of_turns(folded)


def nt(a, b):
    return lax.dot_general(a, b, (((1,), (1,)), ((), ())), preferred_element_type=F32)


def kernel(
    waves, levels, fields, rows, modes,
    order_smem, pair_smem, nlon_smem, gauss_smem, spec_ref, leg_hbm, lanes_ref,
    grid_ref, tend_ref,
    leg, cube, flat, send_a, recv_a, near_c, near_s, far, turned,
    send_f, recv_f, flat_p, send_p, recv_p, turned_p, total, send_d, recv_d,
    leg_sem, send_sem, recv_sem,
):
    wave = lax.axis_index("wave")
    lev = lax.axis_index("lev")
    chunks = waves // 2
    parts = 2 * fields
    groups = leg_sem.shape[0]
    group_rows = rows // groups

    def leg_copy(g):
        block = pl.ds(g * group_rows, group_rows)
        return pltpu.make_async_copy(leg_hbm.at[block], leg.at[block], leg_sem.at[g])

    for g in range(groups):
        leg_copy(g).start()

    barrier = pltpu.get_barrier_semaphore()

    @pl.loop(1, waves)
    def _(s):
        pl.semaphore_signal(
            barrier, inc=1, device_id={"wave": lax.rem(wave + s, waves)}, device_id_type=MESH
        )

    @pl.loop(1, levels)
    def _(s):
        pl.semaphore_signal(
            barrier, inc=1, device_id={"lev": lax.rem(lev + s, levels)}, device_id_type=MESH
        )

    def exchange(axis, me, count, source, target, index):
        @pl.loop(0, count - 1)
        def _(t):
            step = (t + 1) // 2
            there = lax.rem(me + count // 2 + step * (1 - 2 * (t % 2)) + count, count)
            pltpu.make_async_remote_copy(
                src_ref=source.at[there],
                dst_ref=target.at[me],
                send_sem=send_sem.at[index],
                recv_sem=recv_sem.at[index],
                device_id={axis: there},
                device_id_type=MESH,
            ).start()

        target[me] = source[me]

    def arrived(count, target, index):
        all_but_one = target.at[pl.ds(0, count - 1)]
        pltpu.make_async_copy(all_but_one, all_but_one, recv_sem.at[index]).wait()

    def left(count, source, index):
        all_but_one = source.at[pl.ds(0, count - 1)]
        pltpu.make_async_copy(all_but_one, all_but_one, send_sem.at[index]).wait()

    cube[...] = jnp.zeros_like(cube)
    degree = lax.broadcasted_iota(jnp.int32, (8, modes), 1)
    sign = (1 - 2 * (degree % 2)).astype(F32)

    def forward_row(r):
        order = order_smem[wave * rows + r]
        turn = (1 - 2 * (order % 2)).astype(F32)
        north = jnp.where(degree >= order, spec_ref[r].astype(F32), 0.0)
        south = north * (sign * turn)
        both = jnp.concatenate([north, south], axis=0).astype(BF16)
        sums = nt(both, leg[r])
        cube[pl.ds(pl.multiple_of(r * 8, 8), 8), : sums.shape[1]] = sums[:8]
        cube[pl.ds(pl.multiple_of((HALF + r) * 8, 8), 8), : sums.shape[1]] = sums[8:]

    per_group = group_rows // ROWS_AT_ONCE
    for g in range(groups):
        leg_copy(g).wait()

        @pl.loop(0, per_group)
        def _(i):
            for k in range(ROWS_AT_ONCE):
                forward_row(g * group_rows + i * ROWS_AT_ONCE + k)

    own_row = lax.broadcasted_iota(jnp.int32, (waves, SEG), 0)
    own_lane = lax.broadcasted_iota(jnp.int32, (waves, SEG), 1)
    held = jnp.zeros((waves, SEG), jnp.int32)
    for i in range(waves):
        held = jnp.where(own_row == i, pair_smem[i], held)
    picker = jnp.where(held == own_lane, 1.0, 0.0).astype(BF16)

    for c in range(8):
        if c < parts:
            block = cube[pl.ds(c, 2 * HALF, stride=8), :].astype(BF16)
            flat[pl.ds(c, waves, stride=8), :] = nt(picker, block)
        else:
            flat[pl.ds(c, waves, stride=8), :] = jnp.zeros((waves, SEG), F32)
    send_a[...] = flat[...].reshape(waves, 8, SEG).astype(BF16)

    pl.semaphore_wait(barrier, waves + levels - 2)
    exchange("wave", wave, waves, send_a, recv_a, 0)

    pair = pair_smem[wave]
    count = nlon_smem[pair]
    points = jnp.full((1, SEG), count.astype(F32))
    inverse = 1.0 / points
    near_k = lax.broadcasted_iota(jnp.int32, (SEG, SEG), 0).astype(F32)
    far_k = (SEG * lax.broadcasted_iota(jnp.int32, (levels, SEG), 0)).astype(F32)

    @pl.loop(0, chunks)
    def _(j):
        orders = lanes_ref[pl.ds(j, 1), :]
        cosine, sine = unit_circle(near_k * orders, points, inverse)
        near_c[j] = cosine
        near_s[j] = sine
        cosine, sine = unit_circle(far_k * orders, points, inverse)
        both = jnp.concatenate([cosine, -sine], axis=1)
        high = both.astype(BF16).astype(F32)
        far[j] = jnp.concatenate([high, both - high], axis=0).astype(BF16)

    arrived(waves, recv_a, 0)

    first_half = lax.broadcasted_iota(jnp.int32, (8, SEG), 1) < HALF

    @pl.loop(0, chunks)
    def _(j):
        even = recv_a[2 * j].astype(F32)
        odd = recv_a[2 * j + 1].astype(F32)
        inside = jnp.where(2.0 * lanes_ref[pl.ds(j, 1), :] < points, 1.0, 0.0)
        north = jnp.where(first_half, even, pltpu.roll(odd, HALF, 1)) * inside
        south = jnp.where(first_half, pltpu.roll(even, HALF, 1), odd) * inside
        cosine = near_c[j]
        sine = near_s[j]
        for h, half in enumerate((north, south)):
            for f in range(fields):
                real = half[2 * f : 2 * f + 1]
                imag = half[2 * f + 1 : 2 * f + 2]
                turned[h * fields + f, j, :, :SEG] = (real * cosine - imag * sine).astype(BF16)
                turned[h * fields + f, j, :, SEG:] = (real * sine + imag * cosine).astype(BF16)

    longitude = SEG * lax.broadcasted_iota(
        jnp.int32, (levels, SEG), 0
    ) + lax.broadcasted_iota(jnp.int32, (levels, SEG), 1)
    scale = jnp.where(longitude < count, 1.0 / math.sqrt(modes), 0.0)
    for hf in range(parts):
        sums = nt(turned[hf, 0], far[0])
        for j in range(1, chunks):
            sums = sums + nt(turned[hf, j], far[j])
        sums = sums.T
        flat_p[pl.ds(hf, levels, stride=8), :] = (sums[:levels] + sums[levels:]) * scale
    for c in range(parts, 8):
        flat_p[pl.ds(c, levels, stride=8), :] = jnp.zeros((levels, SEG), F32)
    send_f[...] = flat_p[...].reshape(levels, 8, SEG).astype(send_f.dtype)
    exchange("lev", lev, levels, send_f, recv_f, 1)
    arrived(levels, recv_f, 1)

    flat_p[...] = recv_f[...].astype(F32).reshape(levels * 8, SEG)
    level_row = lax.broadcasted_iota(jnp.int32, (levels, levels), 0)
    level_lane = lax.broadcasted_iota(jnp.int32, (levels, levels), 1)
    above = jnp.where(level_lane >= level_row, 1.0, 0.0)
    products = []
    for h in range(2):
        east, north, heat = (
            flat_p[pl.ds(h * fields + f, levels, stride=8), :] for f in range(fields)
        )
        for f, value in enumerate((east, north, heat)):
            grid_ref[h, f] = value
        geopotential = jnp.dot(
            above, heat, precision=lax.Precision.HIGHEST, preferred_element_type=F32
        ) * (1.0 / math.sqrt(levels))
        products += [east * heat, north * heat, east * north + geopotential]
    for hf, value in enumerate(products):
        flat_p[pl.ds(hf, levels, stride=8), :] = value
    send_p[...] = flat_p[...].reshape(levels, 8, SEG).astype(BF16)
    exchange("lev", lev, levels, send_p, recv_p, 2)
    arrived(levels, recv_p, 2)

    flat_p[...] = recv_p[...].astype(F32).reshape(levels * 8, SEG)
    for hf in range(parts):
        block = flat_p[pl.ds(hf, levels, stride=8), :]
        turned_p[hf] = jnp.concatenate([block, block], axis=0).T.astype(BF16)
    total[...] = jnp.zeros_like(total)

    root = lax.rsqrt(points)
    factors = [root * gauss_smem[2 * pair + h] for h in range(2)]

    @pl.loop(0, chunks)
    def _(j):
        cosine = near_c[j]
        sine = near_s[j]
        for h in range(2):
            for f in range(fields):
                inner = jnp.dot(turned_p[h * fields + f], far[j], preferred_element_type=F32)
                even = inner[:, :SEG]
                odd = inner[:, SEG:]
                real = jnp.sum(even * cosine + odd * sine, axis=0, keepdims=True)
                imag = jnp.sum(odd * cosine - even * sine, axis=0, keepdims=True)
                total[h, 2 * f : 2 * f + 1] = real
                total[h, 2 * f + 1 : 2 * f + 2] = imag
        inside = jnp.where(2.0 * lanes_ref[pl.ds(j, 1), :] < points, 1.0, 0.0)
        north = total[0] * (factors[0] * inside)
        south = total[1] * (factors[1] * inside)
        send_d[2 * j] = jnp.where(first_half, north, pltpu.roll(south, HALF, 1)).astype(BF16)
        send_d[2 * j + 1] = jnp.where(first_half, pltpu.roll(north, HALF, 1), south).astype(BF16)

    exchange("wave", wave, waves, send_d, recv_d, 3)
    arrived(waves, recv_d, 3)

    flat[...] = recv_d[...].astype(F32).reshape(waves * 8, SEG)
    for c in range(parts):
        block = flat[pl.ds(c, waves, stride=8), :].astype(BF16)
        cube[pl.ds(c, 2 * HALF, stride=8), :] = lax.dot_general(
            block, picker, (((0,), (0,)), ((), ())), preferred_element_type=F32
        )
    outer = math.sqrt(modes / (2 * waves))

    @pl.loop(0, rows // ROWS_AT_ONCE)
    def _(i):
        for k in range(ROWS_AT_ONCE):
            r = i * ROWS_AT_ONCE + k
            order = order_smem[wave * rows + r]
            turn = (1 - 2 * (order % 2)).astype(F32)
            north = cube[pl.ds(pl.multiple_of(r * 8, 8), 8), :]
            south = cube[pl.ds(pl.multiple_of((HALF + r) * 8, 8), 8), :]
            both = jnp.concatenate([north, south], axis=0)[:, :waves].astype(BF16)
            sums = jnp.dot(both, leg[r], preferred_element_type=F32)
            mixed = (sums[:8] + sums[8:] * (sign * turn)) * outer
            tend_ref[r] = jnp.where(degree >= order, mixed, 0.0).astype(BF16)

    for index, (size, source) in enumerate(
        ((waves, send_a), (levels, send_f), (levels, send_p), (waves, send_d))
    ):
        left(size, source, index)


def local(spectral, legendre, gauss, wave_order, pair_order, nlon):
    rows, _, fields, _, modes = spectral.shape
    waves = lax.axis_size("wave")
    levels = lax.axis_size("lev")
    parts = 2 * fields
    spec = jnp.transpose(spectral, (0, 2, 3, 1, 4)).reshape(rows, parts, modes)
    spec = jnp.pad(spec, ((0, 0), (0, 8 - parts), (0, 0)))
    lanes = jnp.pad(wave_order.reshape(waves, rows), ((0, 0), (0, HALF - rows)))
    lanes = lanes.reshape(waves // 2, SEG).astype(F32)
    vmem = pl.BlockSpec(memory_space=pltpu.VMEM)
    smem = pl.BlockSpec(memory_space=pltpu.SMEM)
    groups = 3 if rows % (3 * ROWS_AT_ONCE) == 0 else 1
    chunks = waves // 2
    scratch = [
        pltpu.VMEM(legendre.shape, BF16),
        pltpu.VMEM((2 * HALF * 8, SEG), F32),
        pltpu.VMEM((waves * 8, SEG), F32),
        pltpu.VMEM((waves, 8, SEG), BF16),
        pltpu.VMEM((waves, 8, SEG), BF16),
        pltpu.VMEM((chunks, SEG, SEG), F32),
        pltpu.VMEM((chunks, SEG, SEG), F32),
        pltpu.VMEM((chunks, 2 * levels, 2 * SEG), BF16),
        pltpu.VMEM((parts, chunks, SEG, 2 * SEG), BF16),
        pltpu.VMEM((levels, 8, SEG), F32),
        pltpu.VMEM((levels, 8, SEG), F32),
        pltpu.VMEM((levels * 8, SEG), F32),
        pltpu.VMEM((levels, 8, SEG), BF16),
        pltpu.VMEM((levels, 8, SEG), BF16),
        pltpu.VMEM((parts, SEG, 2 * levels), BF16),
        pltpu.VMEM((2, 8, SEG), F32),
        pltpu.VMEM((waves, 8, SEG), BF16),
        pltpu.VMEM((waves, 8, SEG), BF16),
        pltpu.SemaphoreType.DMA((groups,)),
        pltpu.SemaphoreType.DMA((4,)),
        pltpu.SemaphoreType.DMA((4,)),
    ]
    grid, tend = pl.pallas_call(
        functools.partial(kernel, waves, levels, fields, rows, modes),
        out_shape=(
            jax.ShapeDtypeStruct((2, fields, levels, SEG), F32),
            jax.ShapeDtypeStruct((rows, 8, modes), BF16),
        ),
        in_specs=[smem, smem, smem, smem, vmem, pl.BlockSpec(memory_space=pl.ANY), vmem],
        out_specs=(vmem, vmem),
        scratch_shapes=scratch,
        compiler_params=pltpu.CompilerParams(collective_id=0, has_side_effects=True),
    )(wave_order, pair_order, nlon, gauss, spec, legendre, lanes)
    tend = tend[:, :parts].reshape(rows, fields, 1, 2, modes)
    return grid, jnp.transpose(tend, (0, 3, 1, 2, 4))


def solution(mesh):
    in_specs = (P("wave", None, None, "lev", None), P("wave", None, None), P(), P(), P(), P())
    out_specs = (P("wave", None, None, "lev"), P("wave", None, None, "lev", None))
    return jax.shard_map(local, mesh=mesh, in_specs=in_specs, out_specs=out_specs, check_vma=False)
```

```python
import functools
import math

import jax
import jax.numpy as jnp
from jax import lax
from jax.experimental import pallas as pl
from jax.experimental.pallas import tpu as pltpu
from jax.sharding import PartitionSpec as P

BF16 = jnp.bfloat16
F32 = jnp.float32
MESH = pl.DeviceIdType.MESH
SEG = 128
VMEM_LIMIT = 24 * 2**20
HALF = 64
NEAR = 32
ROWS_AT_ONCE = 9
CHUNKS_AT_ONCE = 2
SERIES = [(-1.0) ** i * (2.0 * math.pi) ** (2 * i + 1) / math.factorial(2 * i + 1) for i in range(6)]


def sine_of_turns(t):
    square = t * t
    total = jnp.full_like(t, SERIES[-1])
    for factor in SERIES[-2::-1]:
        total = total * square + factor
    return total * t


def unit_circle(product, points, inverse):
    t = (product - jnp.floor(product * inverse + 0.5) * points) * inverse
    folded = jnp.where(t > 0.25, 0.5 - t, jnp.where(t < -0.25, -0.5 - t, t))
    return sine_of_turns(0.25 - jnp.abs(t)), sine_of_turns(folded)


def nt(a, b):
    return lax.dot_general(a, b, (((1,), (1,)), ((), ())), preferred_element_type=F32)


def one_hot(order, size):
    row = lax.broadcasted_iota(jnp.int32, (size, SEG), 0)
    lane = lax.broadcasted_iota(jnp.int32, (size, SEG), 1)
    held = jnp.zeros((size, SEG), jnp.int32)
    for i in range(size):
        held = jnp.where(row == i, order[i], held)
    return jnp.where(held == lane, 1.0, 0.0).astype(BF16)


def kernel(
    waves, levels, fields, rows, modes,
    order_hbm, pair_hbm, nlon_hbm, gauss_hbm, spec_hbm, leg_hbm,
    grid_ref, recv_d, picker_ref, own_ref,
    order_smem, pair_smem, nlon_smem, gauss_smem, order_row, lanes_ref, spec,
    leg, cube, flat, send_a, recv_a, near_c, near_s, far, turned,
    send_f, recv_f, flat_p, send_p, recv_p, turned_p, total, send_d,
    small_sem, leg_sem, spec_sem, out_sem, send_sem, recv_sem,
):
    wave = lax.axis_index("wave")
    lev = lax.axis_index("lev")
    chunks = waves // 2
    parts = 2 * fields
    groups = leg_sem.shape[0]
    group_rows = rows // groups

    def leg_copy(g):
        block = pl.ds(g * group_rows, group_rows)
        return pltpu.make_async_copy(leg_hbm.at[block], leg.at[block], leg_sem.at[g])

    def spec_copy(g):
        block = pl.ds(g * group_rows, group_rows)
        return pltpu.make_async_copy(spec_hbm.at[block], spec.at[block], spec_sem.at[g])

    small = [
        pltpu.make_async_copy(order_hbm, order_smem, small_sem.at[0]),
        pltpu.make_async_copy(pair_hbm, pair_smem, small_sem.at[1]),
        pltpu.make_async_copy(nlon_hbm, nlon_smem, small_sem.at[2]),
        pltpu.make_async_copy(gauss_hbm, gauss_smem, small_sem.at[3]),
        pltpu.make_async_copy(order_hbm, order_row.at[0], small_sem.at[4]),
    ]
    for copy in small:
        copy.start()
    for g in range(groups):
        spec_copy(g).start()
        leg_copy(g).start()

    barrier = pltpu.get_barrier_semaphore()

    def wrapped(me, step, count):
        return jnp.where(me + step >= count, me + step - count, me + step)

    def far_first(count):
        return sorted(range(1, count), key=lambda s: -min(s, count - s))

    for axis, me, size in (("wave", wave, waves), ("lev", lev, levels)):
        for step in far_first(size):
            pl.semaphore_signal(
                barrier, inc=1, device_id={axis: wrapped(me, step, size)}, device_id_type=MESH
            )

    def exchange(axis, me, count, source, target, index):
        for step in far_first(count):
            there = wrapped(me, step, count)
            pltpu.make_async_remote_copy(
                src_ref=source.at[there],
                dst_ref=target.at[me],
                send_sem=send_sem.at[index],
                recv_sem=recv_sem.at[index],
                device_id={axis: there},
                device_id_type=MESH,
            ).start()

        if index < 3:
            target[me] = source[me]
        else:
            pltpu.make_async_copy(source.at[me], target.at[me], out_sem.at[0]).start()

    def arrived(count, target, index):
        all_but_one = target.at[pl.ds(0, count - 1)]
        pltpu.make_async_copy(all_but_one, all_but_one, recv_sem.at[index]).wait()

    def left(count, source, index):
        all_but_one = source.at[pl.ds(0, count - 1)]
        pltpu.make_async_copy(all_but_one, all_but_one, send_sem.at[index]).wait()

    cube[...] = jnp.zeros_like(cube)
    for copy in small:
        copy.wait()
    degree = lax.broadcasted_iota(jnp.int32, (8, modes), 1)
    padding = jnp.zeros((8 - parts, modes), F32)
    sign = (1 - 2 * (degree % 2)).astype(F32)

    def forward_row(r):
        order = order_smem[wave * rows + r]
        turn = (1 - 2 * (order % 2)).astype(F32)
        north = jnp.where(degree >= order, jnp.concatenate([spec[r].astype(F32).reshape(parts, modes), padding], axis=0), 0.0)
        south = north * (sign * turn)
        both = jnp.concatenate([north, south], axis=0).astype(BF16)
        sums = nt(both, leg[r])
        cube[pl.ds(pl.multiple_of(r * 8, 8), 8), : sums.shape[1]] = sums[:8]
        cube[pl.ds(pl.multiple_of((HALF + r) * 8, 8), 8), : sums.shape[1]] = sums[8:]

    per_group = group_rows // ROWS_AT_ONCE
    for g in range(groups):
        spec_copy(g).wait()
        leg_copy(g).wait()

        @pl.loop(0, per_group)
        def _(i):
            for k in range(ROWS_AT_ONCE):
                forward_row(g * group_rows + i * ROWS_AT_ONCE + k)

    picker = one_hot(pair_smem, waves)
    for c in range(8):
        if c < parts:
            block = cube[pl.ds(c, 2 * HALF, stride=8), :].astype(BF16)
            flat[pl.ds(c, waves, stride=8), :] = nt(picker, block)
        else:
            flat[pl.ds(c, waves, stride=8), :] = jnp.zeros((waves, SEG), F32)
    send_a[...] = flat[...].reshape(waves, 8, SEG).astype(BF16)

    pl.semaphore_wait(barrier, waves + levels - 2)
    exchange("wave", wave, waves, send_a, recv_a, 0)

    picker_ref[...] = picker
    for r in range(rows):
        own_ref[r : r + 1, :] = jnp.full((1, SEG), order_smem[wave * rows + r].astype(F32))
    gap = jnp.zeros((1, HALF - rows), F32)
    for j in range(chunks):
        first = order_row[:, 2 * j * rows : (2 * j + 1) * rows].astype(F32)
        second = order_row[:, (2 * j + 1) * rows : (2 * j + 2) * rows].astype(F32)
        lanes_ref[j : j + 1, :] = jnp.concatenate([first, gap, second, gap], axis=1)

    pair = pair_smem[wave]
    count = nlon_smem[pair]
    points = jnp.full((1, SEG), count.astype(F32))
    inverse = 1.0 / points
    near_k = lax.broadcasted_iota(jnp.int32, (NEAR, SEG), 0).astype(F32)
    segment = SEG * lax.broadcasted_iota(jnp.int32, (levels, SEG), 0)
    far_k = jnp.concatenate([segment + s for s in range(0, SEG, NEAR)], axis=0).astype(F32)

    @pl.loop(0, chunks)
    def _(j):
        orders = lanes_ref[pl.ds(j, 1), :]
        cosine, sine = unit_circle(near_k * orders, points, inverse)
        near_c[j] = cosine
        near_s[j] = sine
        cosine, sine = unit_circle(far_k * orders, points, inverse)
        both = jnp.concatenate([cosine, -sine], axis=1)
        high = both.astype(BF16).astype(F32)
        far[:, pl.ds(pl.multiple_of(j * 2 * SEG, SEG), 2 * SEG)] = jnp.concatenate(
            [high, both - high], axis=0
        ).astype(BF16)

    arrived(waves, recv_a, 0)

    first_half = lax.broadcasted_iota(jnp.int32, (8, SEG), 1) < HALF

    def turn_chunk(j):
        even = recv_a[2 * j].astype(F32)
        odd = recv_a[2 * j + 1].astype(F32)
        inside = jnp.where(2.0 * lanes_ref[pl.ds(j, 1), :] < points, 1.0, 0.0)
        north = jnp.where(first_half, even, pltpu.roll(odd, HALF, 1)) * inside
        south = jnp.where(first_half, pltpu.roll(even, HALF, 1), odd) * inside
        cosine = near_c[j]
        sine = near_s[j]
        first = pl.ds(pl.multiple_of(j * 2 * SEG, SEG), SEG)
        second = pl.ds(pl.multiple_of(j * 2 * SEG + SEG, SEG), SEG)
        for h, half in enumerate((north, south)):
            for f in range(fields):
                real = half[2 * f : 2 * f + 1]
                imag = half[2 * f + 1 : 2 * f + 2]
                place = slice((h * fields + f) * NEAR, (h * fields + f + 1) * NEAR)
                turned[place, first] = (real * cosine - imag * sine).astype(BF16)
                turned[place, second] = (real * sine + imag * cosine).astype(BF16)

    @pl.loop(0, chunks // CHUNKS_AT_ONCE)
    def _(i):
        for k in range(CHUNKS_AT_ONCE):
            turn_chunk(i * CHUNKS_AT_ONCE + k)

    splits = SEG // NEAR
    quarter = lax.broadcasted_iota(jnp.int32, (levels, SEG), 1) // NEAR

    def swap(blocks):
        results = []
        for p in range(splits):
            result = blocks[p]
            for q, block in enumerate(blocks):
                if q != p:
                    moved = pltpu.roll(block, ((q - p) * NEAR) % SEG, 1)
                    result = jnp.where(quarter == q, moved, result)
            results.append(result)
        return results

    longitude = segment + lax.broadcasted_iota(jnp.int32, (levels, SEG), 1)
    scale = jnp.where(longitude < count, 1.0 / math.sqrt(modes), 0.0)
    sums = nt(turned[...], far[...])
    sums = sums[:, : splits * levels] + sums[:, splits * levels :]
    for first in range(0, parts, splits):
        held_parts = min(splits, parts - first)
        block = sums[first * NEAR : (first + held_parts) * NEAR]
        if held_parts < splits:
            block = jnp.concatenate(
                [block, jnp.zeros((SEG - block.shape[0], block.shape[1]), F32)], axis=0
            )
        block = block.T
        blocks = swap([block[q * levels : (q + 1) * levels] for q in range(splits)])
        for p in range(held_parts):
            flat_p[pl.ds(first + p, levels, stride=8), :] = blocks[p] * scale
    for c in range(parts, 8):
        flat_p[pl.ds(c, levels, stride=8), :] = jnp.zeros((levels, SEG), F32)
    send_f[...] = flat_p[...].reshape(levels, 8, SEG).astype(send_f.dtype)
    exchange("lev", lev, levels, send_f, recv_f, 1)
    arrived(levels, recv_f, 1)

    flat_p[...] = recv_f[...].astype(F32).reshape(levels * 8, SEG)
    level_row = lax.broadcasted_iota(jnp.int32, (levels, levels), 0)
    level_lane = lax.broadcasted_iota(jnp.int32, (levels, levels), 1)
    above = jnp.where(level_lane >= level_row, 1.0, 0.0)
    products = []
    for h in range(2):
        east, north, heat = (
            flat_p[pl.ds(h * fields + f, levels, stride=8), :] for f in range(fields)
        )
        for f, value in enumerate((east, north, heat)):
            grid_ref[h, f] = value
        geopotential = jnp.dot(
            above, heat, precision=lax.Precision.HIGHEST, preferred_element_type=F32
        ) * (1.0 / math.sqrt(levels))
        products += [east * heat, north * heat, east * north + geopotential]
    for hf, value in enumerate(products):
        flat_p[pl.ds(hf, levels, stride=8), :] = value
    send_p[...] = flat_p[...].reshape(levels, 8, SEG).astype(BF16)
    exchange("lev", lev, levels, send_p, recv_p, 2)
    arrived(levels, recv_p, 2)

    flat_p[...] = recv_p[...].astype(F32).reshape(levels * 8, SEG)
    for first in range(0, parts, splits):
        held_parts = min(splits, parts - first)
        blocks = [flat_p[pl.ds(first + p, levels, stride=8), :] for p in range(held_parts)]
        blocks += [jnp.zeros((levels, SEG), F32)] * (splits - held_parts)
        block = jnp.concatenate(swap(blocks), axis=0).T[: held_parts * NEAR]
        turned_p[first * NEAR : (first + held_parts) * NEAR] = jnp.concatenate(
            [block, block], axis=1
        ).astype(BF16)
    total[...] = jnp.zeros_like(total)

    root = lax.rsqrt(points)
    factors = [root * gauss_smem[2 * pair + h] for h in range(2)]

    def return_chunk(j, total):
        cosine = near_c[j]
        sine = near_s[j]
        inner = jnp.dot(
            turned_p[...],
            far[:, pl.ds(pl.multiple_of(j * 2 * SEG, SEG), 2 * SEG)],
            preferred_element_type=F32,
        )
        for h in range(2):
            for f in range(fields):
                place = slice((h * fields + f) * NEAR, (h * fields + f + 1) * NEAR)
                even = inner[place, :SEG]
                odd = inner[place, SEG:]
                real = jnp.sum(even * cosine + odd * sine, axis=0, keepdims=True)
                imag = jnp.sum(odd * cosine - even * sine, axis=0, keepdims=True)
                total[h, 2 * f : 2 * f + 1] = real
                total[h, 2 * f + 1 : 2 * f + 2] = imag
        inside = jnp.where(2.0 * lanes_ref[pl.ds(j, 1), :] < points, 1.0, 0.0)
        north = total[0] * (factors[0] * inside)
        south = total[1] * (factors[1] * inside)
        send_d[2 * j] = jnp.where(first_half, north, pltpu.roll(south, HALF, 1)).astype(BF16)
        send_d[2 * j + 1] = jnp.where(first_half, pltpu.roll(north, HALF, 1), south).astype(BF16)

    @pl.loop(0, chunks // CHUNKS_AT_ONCE)
    def _(i):
        for k in range(CHUNKS_AT_ONCE):
            return_chunk(i * CHUNKS_AT_ONCE + k, total.at[k])

    exchange("wave", wave, waves, send_d, recv_d, 3)
    arrived(waves, recv_d, 3)

    pltpu.make_async_copy(send_d.at[wave], recv_d.at[wave], out_sem.at[0]).wait()

    for index, (size, source) in enumerate(
        ((waves, send_a), (levels, send_f), (levels, send_p), (waves, send_d))
    ):
        left(size, source, index)


def back_kernel(
    waves, fields, rows, modes,
    recv, picker_ref, own_ref, grid, leg,
    grid_hbm, tend_hbm,
    tend, flat, cube, out_sem,
):
    parts = 2 * fields
    groups = out_sem.shape[0] - 1
    group_rows = rows // groups

    def tend_copy(g):
        block = pl.ds(g * group_rows, group_rows)
        return pltpu.make_async_copy(tend.at[block], tend_hbm.at[block], out_sem.at[g])

    grid_copy = pltpu.make_async_copy(grid, grid_hbm, out_sem.at[groups])
    grid_copy.start()
    degree = lax.broadcasted_iota(jnp.int32, (8, modes), 1)
    sign = (1 - 2 * (degree % 2)).astype(F32)
    place = degree.astype(F32)
    outer = math.sqrt(modes / (2 * waves))
    picker = picker_ref[...]
    flat[...] = recv[...].astype(F32).reshape(waves * 8, SEG)
    for c in range(parts):
        block = flat[pl.ds(c, waves, stride=8), :].astype(BF16)
        cube[pl.ds(c, 2 * HALF, stride=8), :] = lax.dot_general(
            block, picker, (((0,), (0,)), ((), ())), preferred_element_type=F32
        )
    for c in range(parts, 8):
        cube[pl.ds(c, 2 * HALF, stride=8), :] = jnp.zeros((2 * HALF, SEG), F32)

    def backward_row(r):
        order = own_ref[pl.ds(r, 1), :1]
        turn = 1.0 - 2.0 * (order - 2.0 * jnp.floor(0.5 * order))
        north = cube[pl.ds(pl.multiple_of(r * 8, 8), 8), :]
        south = cube[pl.ds(pl.multiple_of((HALF + r) * 8, 8), 8), :]
        both = jnp.concatenate([north, south], axis=0)[:, :waves].astype(BF16)
        sums = jnp.dot(both, leg[r], preferred_element_type=F32)
        mixed = (sums[:8] + sums[8:] * (sign * turn)) * outer
        mixed = jnp.where(place >= order, mixed, 0.0).astype(BF16)
        tend[r] = mixed.reshape(4, 2, modes)[:fields]

    for g in range(groups):

        @pl.loop(0, group_rows // ROWS_AT_ONCE)
        def _(i):
            for k in range(ROWS_AT_ONCE):
                backward_row(g * group_rows + i * ROWS_AT_ONCE + k)

        tend_copy(g).start()

    for g in range(groups):
        tend_copy(g).wait()
    grid_copy.wait()


def local(spectral, legendre, gauss, wave_order, pair_order, nlon):
    rows, _, fields, _, modes = spectral.shape
    waves = lax.axis_size("wave")
    levels = lax.axis_size("lev")
    parts = 2 * fields
    spec = jnp.transpose(spectral, (0, 2, 3, 1, 4)).reshape(rows, fields, 2, modes)
    anywhere = pl.BlockSpec(memory_space=pl.ANY)
    groups = max(g for g in (1, 2, 3, 6) if rows % (g * ROWS_AT_ONCE) == 0)
    chunks = waves // 2
    scratch = [
        pltpu.SMEM(wave_order.shape, jnp.int32),
        pltpu.SMEM(pair_order.shape, jnp.int32),
        pltpu.SMEM(nlon.shape, jnp.int32),
        pltpu.SMEM(gauss.shape, F32),
        pltpu.VMEM((1, *wave_order.shape), jnp.int32),
        pltpu.VMEM((chunks, SEG), F32),
        pltpu.VMEM(spec.shape, BF16),
        pltpu.VMEM(legendre.shape, BF16),
        pltpu.VMEM((2 * HALF * 8, SEG), F32),
        pltpu.VMEM((waves * 8, SEG), F32),
        pltpu.VMEM((waves, 8, SEG), BF16),
        pltpu.VMEM((waves, 8, SEG), BF16),
        pltpu.VMEM((chunks, NEAR, SEG), F32),
        pltpu.VMEM((chunks, NEAR, SEG), F32),
        pltpu.VMEM((2 * levels * SEG // NEAR, chunks * 2 * SEG), BF16),
        pltpu.VMEM((parts * NEAR, chunks * 2 * SEG), BF16),
        pltpu.VMEM((levels, 8, SEG), F32),
        pltpu.VMEM((levels, 8, SEG), F32),
        pltpu.VMEM((levels * 8, SEG), F32),
        pltpu.VMEM((levels, 8, SEG), BF16),
        pltpu.VMEM((levels, 8, SEG), BF16),
        pltpu.VMEM((parts * NEAR, 2 * levels * SEG // NEAR), BF16),
        pltpu.VMEM((CHUNKS_AT_ONCE, 2, 8, SEG), F32),
        pltpu.VMEM((waves, 8, SEG), BF16),
        pltpu.SemaphoreType.DMA((5,)),
        pltpu.SemaphoreType.DMA((groups,)),
        pltpu.SemaphoreType.DMA((groups,)),
        pltpu.SemaphoreType.DMA((1,)),
        pltpu.SemaphoreType.DMA((4,)),
        pltpu.SemaphoreType.DMA((4,)),
    ]
    inputs = (wave_order, pair_order, nlon, gauss, spec, legendre)
    grid_shape = jax.ShapeDtypeStruct((2, fields, levels, SEG), F32)
    far_memory = pl.BlockSpec(memory_space=pltpu.HBM)
    vmem = pl.BlockSpec(memory_space=pltpu.VMEM)
    grid, weighted, picker, own = pl.pallas_call(
        functools.partial(kernel, waves, levels, fields, rows, modes),
        out_shape=(
            grid_shape,
            jax.ShapeDtypeStruct((waves, 8, SEG), BF16),
            jax.ShapeDtypeStruct((waves, SEG), BF16),
            jax.ShapeDtypeStruct((rows, SEG), F32),
        ),
        in_specs=[far_memory] * 6,
        out_specs=(vmem, anywhere, vmem, vmem),
        scratch_shapes=scratch,
        compiler_params=pltpu.CompilerParams(
            collective_id=0, has_side_effects=True, vmem_limit_bytes=VMEM_LIMIT
        ),
    )(*(pltpu.with_memory_space_constraint(x, pltpu.HBM) for x in inputs))
    grid, tend = pl.pallas_call(
        functools.partial(back_kernel, waves, fields, rows, modes),
        out_shape=(grid_shape, jax.ShapeDtypeStruct(spec.shape, BF16)),
        in_specs=[vmem] * 5,
        out_specs=(anywhere, anywhere),
        scratch_shapes=[
            pltpu.VMEM(spec.shape, BF16),
            pltpu.VMEM((waves * 8, SEG), F32),
            pltpu.VMEM((2 * HALF * 8, SEG), F32),
            pltpu.SemaphoreType.DMA((groups + 1,)),
        ],
        compiler_params=pltpu.CompilerParams(vmem_limit_bytes=VMEM_LIMIT),
    )(weighted, picker, own, grid, legendre)
    tend = tend.reshape(rows, fields, 1, 2, modes)
    return grid, jnp.transpose(tend, (0, 3, 1, 2, 4))


def solution(mesh):
    in_specs = (P("wave", None, None, "lev", None), P("wave", None, None), P(), P(), P(), P())
    out_specs = (P("wave", None, None, "lev"), P("wave", None, None, "lev", None))
    return jax.shard_map(local, mesh=mesh, in_specs=in_specs, out_specs=out_specs, check_vma=False)
```

```python
import functools
import math

import jax
import jax.numpy as jnp
from jax import lax
from jax.experimental import pallas as pl
from jax.experimental.pallas import tpu as pltpu
from jax.sharding import PartitionSpec as P

BF16 = jnp.bfloat16
F32 = jnp.float32
MESH = pl.DeviceIdType.MESH
SEG = 128
VMEM_LIMIT = 24 * 2**20
HALF = 64
NEAR = 32
ROWS_AT_ONCE = 9
SERIES = [(-1.0) ** i * (2.0 * math.pi) ** (2 * i + 1) / math.factorial(2 * i + 1) for i in range(6)]


def sine_of_turns(t):
    square = t * t
    total = jnp.full_like(t, SERIES[-1])
    for factor in SERIES[-2::-1]:
        total = total * square + factor
    return total * t


def unit_circle(product, points, inverse):
    t = (product - jnp.floor(product * inverse + 0.5) * points) * inverse
    folded = jnp.where(t > 0.25, 0.5 - t, jnp.where(t < -0.25, -0.5 - t, t))
    return sine_of_turns(0.25 - jnp.abs(t)), sine_of_turns(folded)


def nt(a, b):
    return lax.dot_general(a, b, (((1,), (1,)), ((), ())), preferred_element_type=F32)


def one_hot(order, size):
    row = lax.broadcasted_iota(jnp.int32, (size, SEG), 0)
    lane = lax.broadcasted_iota(jnp.int32, (size, SEG), 1)
    held = jnp.zeros((size, SEG), jnp.int32)
    for i in range(size):
        held = jnp.where(row == i, order[i], held)
    return jnp.where(held == lane, 1.0, 0.0).astype(BF16)


def kernel(
    waves, levels, fields, rows, modes,
    order_hbm, pair_hbm, nlon_hbm, gauss_hbm, spec_hbm, leg_hbm,
    grid_ref, recv_d, picker_ref, own_ref,
    order_smem, pair_smem, nlon_smem, gauss_smem, order_row, lanes_ref, spec,
    leg, cube, flat, send_a, recv_a, near_c, near_s, far, turned,
    send_f, recv_f, flat_p, send_p, recv_p, turned_p, total, send_d,
    small_sem, leg_sem, spec_sem, out_sem, send_sem, recv_sem,
):
    wave = lax.axis_index("wave")
    lev = lax.axis_index("lev")
    chunks = waves // 2
    parts = 2 * fields
    groups = leg_sem.shape[0]
    group_rows = rows // groups

    def leg_copy(g):
        block = pl.ds(g * group_rows, group_rows)
        return pltpu.make_async_copy(leg_hbm.at[block], leg.at[block], leg_sem.at[g])

    def spec_copy(g):
        block = pl.ds(g * group_rows, group_rows)
        return pltpu.make_async_copy(spec_hbm.at[block], spec.at[block], spec_sem.at[g])

    small = [
        pltpu.make_async_copy(order_hbm, order_smem, small_sem.at[0]),
        pltpu.make_async_copy(pair_hbm, pair_smem, small_sem.at[1]),
        pltpu.make_async_copy(nlon_hbm, nlon_smem, small_sem.at[2]),
        pltpu.make_async_copy(gauss_hbm, gauss_smem, small_sem.at[3]),
        pltpu.make_async_copy(order_hbm, order_row.at[0], small_sem.at[4]),
    ]
    for copy in small:
        copy.start()
    for g in range(groups):
        spec_copy(g).start()
        leg_copy(g).start()

    barrier = pltpu.get_barrier_semaphore()

    def wrapped(me, step, count):
        return jnp.where(me + step >= count, me + step - count, me + step)

    def hops(step, count):
        return min(step, count - step)

    across = 4 if levels % 4 == 0 else 1
    down = levels // across
    lev_y = lev // across
    lev_x = lev % across
    cores = 2
    peers = {"wave": [], "lev": []}
    for step in range(1, waves):
        peers["wave"].append((hops(step, waves) / cores, wrapped(wave, step, waves)))
    for dy in range(down):
        for dx in range(across):
            if dy or dx:
                there = wrapped(lev_y, dy, down) * across + wrapped(lev_x, dx, across)
                peers["lev"].append((hops(dy, down) + hops(dx, across), there))
    for axis in peers:
        peers[axis].sort(key=lambda peer: -peer[0])
    greeted = [(far, axis, there) for axis in peers for far, there in peers[axis]]
    for _, axis, there in sorted(greeted, key=lambda peer: -peer[0]):
        pl.semaphore_signal(barrier, inc=1, device_id={axis: there}, device_id_type=MESH)

    def exchange(axis, me, count, source, target, index):
        for _, there in peers[axis]:
            pltpu.make_async_remote_copy(
                src_ref=source.at[there],
                dst_ref=target.at[me],
                send_sem=send_sem.at[index],
                recv_sem=recv_sem.at[index],
                device_id={axis: there},
                device_id_type=MESH,
            ).start()

        if index < 3:
            target[me] = source[me]
        else:
            pltpu.make_async_copy(source.at[me], target.at[me], out_sem.at[0]).start()

    def arrived(count, target, index):
        all_but_one = target.at[pl.ds(0, count - 1)]
        pltpu.make_async_copy(all_but_one, all_but_one, recv_sem.at[index]).wait()

    def left(count, source, index):
        all_but_one = source.at[pl.ds(0, count - 1)]
        pltpu.make_async_copy(all_but_one, all_but_one, send_sem.at[index]).wait()

    cube[...] = jnp.zeros_like(cube)
    for copy in small:
        copy.wait()
    degree = lax.broadcasted_iota(jnp.int32, (8, modes), 1)
    padding = jnp.zeros((8 - parts, modes), F32)
    sign = (1 - 2 * (degree % 2)).astype(F32)

    def forward_row(r):
        order = order_smem[wave * rows + r]
        turn = (1 - 2 * (order % 2)).astype(F32)
        north = jnp.where(degree >= order, jnp.concatenate([spec[r].astype(F32).reshape(parts, modes), padding], axis=0), 0.0)
        south = north * sign
        both = jnp.concatenate([north, south], axis=0).astype(BF16)
        sums = nt(both, leg[r])
        cube[pl.ds(pl.multiple_of(r * 8, 8), 8), : sums.shape[1]] = sums[:8]
        cube[pl.ds(pl.multiple_of((HALF + r) * 8, 8), 8), : sums.shape[1]] = sums[8:] * turn

    per_group = group_rows // ROWS_AT_ONCE
    for g in range(groups):
        spec_copy(g).wait()
        leg_copy(g).wait()

        @pl.loop(0, per_group)
        def _(i):
            for k in range(ROWS_AT_ONCE):
                forward_row(g * group_rows + i * ROWS_AT_ONCE + k)

    picker = one_hot(pair_smem, waves)
    for c in range(8):
        if c < parts:
            block = cube[pl.ds(c, 2 * HALF, stride=8), :].astype(BF16)
            flat[pl.ds(c, waves, stride=8), :] = nt(picker, block)
        else:
            flat[pl.ds(c, waves, stride=8), :] = jnp.zeros((waves, SEG), F32)
    send_a[...] = flat[...].reshape(waves, 8, SEG).astype(BF16)

    pl.semaphore_wait(barrier, waves + levels - 2)
    exchange("wave", wave, waves, send_a, recv_a, 0)

    picker_ref[...] = picker
    for r in range(rows):
        own_ref[r : r + 1, :] = jnp.full((1, SEG), order_smem[wave * rows + r].astype(F32))
    gap = jnp.zeros((1, HALF - rows), F32)
    for j in range(chunks):
        first = order_row[:, 2 * j * rows : (2 * j + 1) * rows].astype(F32)
        second = order_row[:, (2 * j + 1) * rows : (2 * j + 2) * rows].astype(F32)
        lanes_ref[j : j + 1, :] = jnp.concatenate([first, gap, second, gap], axis=1)

    pair = pair_smem[wave]
    count = nlon_smem[pair]
    points = jnp.full((1, SEG), count.astype(F32))
    inverse = 1.0 / points
    near_k = lax.broadcasted_iota(jnp.int32, (NEAR, SEG), 0).astype(F32)
    segment = SEG * lax.broadcasted_iota(jnp.int32, (levels, SEG), 0)
    far_k = jnp.concatenate([segment + s for s in range(0, SEG, NEAR)], axis=0).astype(F32)

    @pl.loop(0, chunks)
    def _(j):
        orders = lanes_ref[pl.ds(j, 1), :]
        cosine, sine = unit_circle(near_k * orders, points, inverse)
        near_c[j] = cosine
        near_s[j] = sine
        cosine, sine = unit_circle(far_k * orders, points, inverse)
        both = jnp.concatenate([cosine, -sine], axis=1)
        high = both.astype(BF16).astype(F32)
        far[:, pl.ds(pl.multiple_of(j * 2 * SEG, SEG), 2 * SEG)] = jnp.concatenate(
            [high, both - high], axis=0
        ).astype(BF16)

    arrived(waves, recv_a, 0)

    first_half = lax.broadcasted_iota(jnp.int32, (8, SEG), 1) < HALF

    def turn_chunk(j):
        even = recv_a[2 * j].astype(F32)
        odd = recv_a[2 * j + 1].astype(F32)
        inside = jnp.where(2.0 * lanes_ref[pl.ds(j, 1), :] < points, 1.0, 0.0)
        north = jnp.where(first_half, even, pltpu.roll(odd, HALF, 1)) * inside
        south = jnp.where(first_half, pltpu.roll(even, HALF, 1), odd) * inside
        cosine = near_c[j]
        sine = near_s[j]
        first = pl.ds(j * 2 * SEG, SEG)
        second = pl.ds(j * 2 * SEG + SEG, SEG)
        for h, half in enumerate((north, south)):
            for f in range(fields):
                real = half[2 * f : 2 * f + 1]
                imag = half[2 * f + 1 : 2 * f + 2]
                place = slice((h * fields + f) * NEAR, (h * fields + f + 1) * NEAR)
                turned[place, first] = (real * cosine - imag * sine).astype(BF16)
                turned[place, second] = (real * sine + imag * cosine).astype(BF16)

    for j in range(chunks):
        turn_chunk(j)

    splits = SEG // NEAR
    quarter = lax.broadcasted_iota(jnp.int32, (levels, SEG), 1) // NEAR

    def swap(blocks):
        results = []
        for p in range(splits):
            result = blocks[p]
            for q, block in enumerate(blocks):
                if q != p:
                    moved = pltpu.roll(block, ((q - p) * NEAR) % SEG, 1)
                    result = jnp.where(quarter == q, moved, result)
            results.append(result)
        return results

    longitude = segment + lax.broadcasted_iota(jnp.int32, (levels, SEG), 1)
    scale = jnp.where(longitude < count, 1.0 / math.sqrt(modes), 0.0)
    sums = nt(turned[...], far[...])
    sums = sums[:, : splits * levels] + sums[:, splits * levels :]
    for first in range(0, parts, splits):
        held_parts = min(splits, parts - first)
        block = sums[first * NEAR : (first + held_parts) * NEAR]
        if held_parts < splits:
            block = jnp.concatenate(
                [block, jnp.zeros((SEG - block.shape[0], block.shape[1]), F32)], axis=0
            )
        block = block.T
        blocks = swap([block[q * levels : (q + 1) * levels] for q in range(splits)])
        for p in range(held_parts):
            flat_p[pl.ds(first + p, levels, stride=8), :] = blocks[p] * scale
    for c in range(parts, 8):
        flat_p[pl.ds(c, levels, stride=8), :] = jnp.zeros((levels, SEG), F32)
    send_f[...] = flat_p[...].reshape(levels, 8, SEG).astype(send_f.dtype)
    exchange("lev", lev, levels, send_f, recv_f, 1)
    arrived(levels, recv_f, 1)

    flat_p[...] = recv_f[...].astype(F32).reshape(levels * 8, SEG)
    level_row = lax.broadcasted_iota(jnp.int32, (levels, levels), 0)
    level_lane = lax.broadcasted_iota(jnp.int32, (levels, levels), 1)
    above = jnp.where(level_lane >= level_row, 1.0, 0.0)
    products = []
    for h in range(2):
        east, north, heat = (
            flat_p[pl.ds(h * fields + f, levels, stride=8), :] for f in range(fields)
        )
        for f, value in enumerate((east, north, heat)):
            grid_ref[h, f] = value
        geopotential = jnp.dot(
            above, heat, precision=lax.Precision.HIGHEST, preferred_element_type=F32
        ) * (1.0 / math.sqrt(levels))
        products += [east * heat, north * heat, east * north + geopotential]
    for hf, value in enumerate(products):
        flat_p[pl.ds(hf, levels, stride=8), :] = value
    send_p[...] = flat_p[...].reshape(levels, 8, SEG).astype(BF16)
    exchange("lev", lev, levels, send_p, recv_p, 2)
    arrived(levels, recv_p, 2)

    flat_p[...] = recv_p[...].astype(F32).reshape(levels * 8, SEG)
    for first in range(0, parts, splits):
        held_parts = min(splits, parts - first)
        blocks = [flat_p[pl.ds(first + p, levels, stride=8), :] for p in range(held_parts)]
        blocks += [jnp.zeros((levels, SEG), F32)] * (splits - held_parts)
        block = jnp.concatenate(swap(blocks), axis=0).T[: held_parts * NEAR]
        turned_p[first * NEAR : (first + held_parts) * NEAR] = jnp.concatenate(
            [block, block], axis=1
        ).astype(BF16)
    total[...] = jnp.zeros_like(total)

    root = lax.rsqrt(points)
    factors = [root * gauss_smem[2 * pair + h] for h in range(2)]

    def return_chunk(j, total):
        cosine = near_c[j]
        sine = near_s[j]
        inner = jnp.dot(
            turned_p[...],
            far[:, pl.ds(j * 2 * SEG, 2 * SEG)],
            preferred_element_type=F32,
        )
        for h in range(2):
            for f in range(fields):
                place = slice((h * fields + f) * NEAR, (h * fields + f + 1) * NEAR)
                even = inner[place, :SEG]
                odd = inner[place, SEG:]
                real = jnp.sum(even * cosine + odd * sine, axis=0, keepdims=True)
                imag = jnp.sum(odd * cosine - even * sine, axis=0, keepdims=True)
                total[h, 2 * f : 2 * f + 1] = real
                total[h, 2 * f + 1 : 2 * f + 2] = imag
        inside = jnp.where(2.0 * lanes_ref[pl.ds(j, 1), :] < points, 1.0, 0.0)
        north = total[0] * (factors[0] * inside)
        south = total[1] * (factors[1] * inside)
        send_d[2 * j] = jnp.where(first_half, north, pltpu.roll(south, HALF, 1)).astype(BF16)
        send_d[2 * j + 1] = jnp.where(first_half, pltpu.roll(north, HALF, 1), south).astype(BF16)

    for j in range(chunks):
        return_chunk(j, total.at[j])

    exchange("wave", wave, waves, send_d, recv_d, 3)
    arrived(waves, recv_d, 3)

    pltpu.make_async_copy(send_d.at[wave], recv_d.at[wave], out_sem.at[0]).wait()

    for index, (size, source) in enumerate(
        ((waves, send_a), (levels, send_f), (levels, send_p), (waves, send_d))
    ):
        left(size, source, index)


def back_kernel(
    waves, fields, rows, modes,
    recv, picker_ref, own_ref, grid, leg,
    grid_hbm, tend_hbm,
    tend, flat, cube, out_sem,
):
    parts = 2 * fields
    groups = out_sem.shape[0] - 1
    group_rows = rows // groups

    def tend_copy(g):
        block = pl.ds(g * group_rows, group_rows)
        return pltpu.make_async_copy(tend.at[block], tend_hbm.at[block], out_sem.at[g])

    grid_copy = pltpu.make_async_copy(grid, grid_hbm, out_sem.at[groups])
    grid_copy.start()
    degree = lax.broadcasted_iota(jnp.int32, (8, modes), 1)
    sign = (1 - 2 * (degree % 2)).astype(F32)
    place = degree.astype(F32)
    outer = math.sqrt(modes / (2 * waves))
    picker = picker_ref[...]
    flat[...] = recv[...].astype(F32).reshape(waves * 8, SEG)
    for c in range(parts):
        block = flat[pl.ds(c, waves, stride=8), :].astype(BF16)
        cube[pl.ds(c, 2 * HALF, stride=8), :] = lax.dot_general(
            block, picker, (((0,), (0,)), ((), ())), preferred_element_type=F32
        )
    for c in range(parts, 8):
        cube[pl.ds(c, 2 * HALF, stride=8), :] = jnp.zeros((2 * HALF, SEG), F32)

    def backward_row(r):
        order = own_ref[pl.ds(r, 1), :1]
        turn = 1.0 - 2.0 * (order - 2.0 * jnp.floor(0.5 * order))
        north = cube[pl.ds(pl.multiple_of(r * 8, 8), 8), :]
        south = cube[pl.ds(pl.multiple_of((HALF + r) * 8, 8), 8), :] * turn
        both = jnp.concatenate([north, south], axis=0)[:, :waves].astype(BF16)
        sums = jnp.dot(both, leg[r], preferred_element_type=F32)
        mixed = (sums[:8] + sums[8:] * sign) * outer
        mixed = jnp.where(place >= order, mixed, 0.0).astype(BF16)
        tend[r] = mixed.reshape(4, 2, modes)[:fields]

    for g in range(groups):

        @pl.loop(0, group_rows // ROWS_AT_ONCE)
        def _(i):
            for k in range(ROWS_AT_ONCE):
                backward_row(g * group_rows + i * ROWS_AT_ONCE + k)

        tend_copy(g).start()

    for g in range(groups):
        tend_copy(g).wait()
    grid_copy.wait()


def local(spectral, legendre, gauss, wave_order, pair_order, nlon):
    rows, _, fields, _, modes = spectral.shape
    waves = lax.axis_size("wave")
    levels = lax.axis_size("lev")
    parts = 2 * fields
    spec = jnp.transpose(spectral, (0, 2, 3, 1, 4)).reshape(rows, fields, 2, modes)
    anywhere = pl.BlockSpec(memory_space=pl.ANY)
    groups = max(g for g in (1, 2, 3, 6) if rows % (g * ROWS_AT_ONCE) == 0)
    chunks = waves // 2
    scratch = [
        pltpu.SMEM(wave_order.shape, jnp.int32),
        pltpu.SMEM(pair_order.shape, jnp.int32),
        pltpu.SMEM(nlon.shape, jnp.int32),
        pltpu.SMEM(gauss.shape, F32),
        pltpu.VMEM((1, *wave_order.shape), jnp.int32),
        pltpu.VMEM((chunks, SEG), F32),
        pltpu.VMEM(spec.shape, BF16),
        pltpu.VMEM(legendre.shape, BF16),
        pltpu.VMEM((2 * HALF * 8, SEG), F32),
        pltpu.VMEM((waves * 8, SEG), F32),
        pltpu.VMEM((waves, 8, SEG), BF16),
        pltpu.VMEM((waves, 8, SEG), BF16),
        pltpu.VMEM((chunks, NEAR, SEG), F32),
        pltpu.VMEM((chunks, NEAR, SEG), F32),
        pltpu.VMEM((2 * levels * SEG // NEAR, chunks * 2 * SEG), BF16),
        pltpu.VMEM((parts * NEAR, chunks * 2 * SEG), BF16),
        pltpu.VMEM((levels, 8, SEG), BF16),
        pltpu.VMEM((levels, 8, SEG), BF16),
        pltpu.VMEM((levels * 8, SEG), F32),
        pltpu.VMEM((levels, 8, SEG), BF16),
        pltpu.VMEM((levels, 8, SEG), BF16),
        pltpu.VMEM((parts * NEAR, 2 * levels * SEG // NEAR), BF16),
        pltpu.VMEM((chunks, 2, 8, SEG), F32),
        pltpu.VMEM((waves, 8, SEG), BF16),
        pltpu.SemaphoreType.DMA((5,)),
        pltpu.SemaphoreType.DMA((groups,)),
        pltpu.SemaphoreType.DMA((groups,)),
        pltpu.SemaphoreType.DMA((1,)),
        pltpu.SemaphoreType.DMA((4,)),
        pltpu.SemaphoreType.DMA((4,)),
    ]
    inputs = (wave_order, pair_order, nlon, gauss, spec, legendre)
    grid_shape = jax.ShapeDtypeStruct((2, fields, levels, SEG), F32)
    far_memory = pl.BlockSpec(memory_space=pltpu.HBM)
    vmem = pl.BlockSpec(memory_space=pltpu.VMEM)
    grid, weighted, picker, own = pl.pallas_call(
        functools.partial(kernel, waves, levels, fields, rows, modes),
        out_shape=(
            grid_shape,
            jax.ShapeDtypeStruct((waves, 8, SEG), BF16),
            jax.ShapeDtypeStruct((waves, SEG), BF16),
            jax.ShapeDtypeStruct((rows, SEG), F32),
        ),
        in_specs=[far_memory] * 6,
        out_specs=(vmem, anywhere, vmem, vmem),
        scratch_shapes=scratch,
        compiler_params=pltpu.CompilerParams(
            collective_id=0, has_side_effects=True, vmem_limit_bytes=VMEM_LIMIT
        ),
    )(*(pltpu.with_memory_space_constraint(x, pltpu.HBM) for x in inputs))
    grid, tend = pl.pallas_call(
        functools.partial(back_kernel, waves, fields, rows, modes),
        out_shape=(grid_shape, jax.ShapeDtypeStruct(spec.shape, BF16)),
        in_specs=[vmem] * 5,
        out_specs=(anywhere, anywhere),
        scratch_shapes=[
            pltpu.VMEM(spec.shape, BF16),
            pltpu.VMEM((waves * 8, SEG), F32),
            pltpu.VMEM((2 * HALF * 8, SEG), F32),
            pltpu.SemaphoreType.DMA((groups + 1,)),
        ],
        compiler_params=pltpu.CompilerParams(vmem_limit_bytes=VMEM_LIMIT),
    )(weighted, picker, own, grid, legendre)
    tend = tend.reshape(rows, fields, 1, 2, modes)
    return grid, jnp.transpose(tend, (0, 3, 1, 2, 4))


def solution(mesh):
    in_specs = (P("wave", None, None, "lev", None), P("wave", None, None), P(), P(), P(), P())
    out_specs = (P("wave", None, None, "lev"), P("wave", None, None, "lev", None))
    return jax.shard_map(local, mesh=mesh, in_specs=in_specs, out_specs=out_specs, check_vma=False)
```

```python
import functools
import math

import jax
import jax.numpy as jnp
from jax import lax
from jax.experimental import pallas as pl
from jax.experimental.pallas import tpu as pltpu
from jax.sharding import PartitionSpec as P

BF16 = jnp.bfloat16
F32 = jnp.float32
MESH = pl.DeviceIdType.MESH
SEG = 128
VMEM_LIMIT = 24 * 2**20
HALF = 64
NEAR = 32
ROWS_AT_ONCE = 9
SERIES = [(-1.0) ** i * (2.0 * math.pi) ** (2 * i + 1) / math.factorial(2 * i + 1) for i in range(6)]


def sine_of_turns(t):
    square = t * t
    total = jnp.full_like(t, SERIES[-1])
    for factor in SERIES[-2::-1]:
        total = total * square + factor
    return total * t


def unit_circle(product, points, inverse):
    t = (product - jnp.floor(product * inverse + 0.5) * points) * inverse
    folded = jnp.where(t > 0.25, 0.5 - t, jnp.where(t < -0.25, -0.5 - t, t))
    return sine_of_turns(0.25 - jnp.abs(t)), sine_of_turns(folded)


def nt(a, b):
    return lax.dot_general(a, b, (((1,), (1,)), ((), ())), preferred_element_type=F32)


def one_hot(order, size):
    row = lax.broadcasted_iota(jnp.int32, (size, SEG), 0)
    lane = lax.broadcasted_iota(jnp.int32, (size, SEG), 1)
    held = jnp.zeros((size, SEG), jnp.int32)
    for i in range(size):
        held = jnp.where(row == i, order[i], held)
    return jnp.where(held == lane, 1.0, 0.0).astype(BF16)


def kernel(
    waves, levels, fields, rows, modes,
    order_hbm, pair_hbm, nlon_hbm, gauss_hbm, spec_hbm, leg_hbm,
    grid_ref, recv_d, picker_ref, own_ref, leg,
    order_smem, pair_smem, nlon_smem, gauss_smem, order_row, lanes_ref, spec,
    cube, flat, send_a, recv_a, near_c, near_s, far, turned,
    send_f, recv_f, flat_p, send_p, recv_p, turned_p, total, send_d,
    small_sem, leg_sem, spec_sem, out_sem, send_sem, recv_sem,
):
    wave = lax.axis_index("wave")
    lev = lax.axis_index("lev")
    chunks = waves // 2
    parts = 2 * fields
    groups = leg_sem.shape[0]
    group_rows = rows // groups

    def leg_copy(g):
        block = pl.ds(g * group_rows, group_rows)
        return pltpu.make_async_copy(leg_hbm.at[block], leg.at[block], leg_sem.at[g])

    def spec_copy(g):
        block = pl.ds(g * group_rows, group_rows)
        return pltpu.make_async_copy(
            spec_hbm.at[block], spec.at[block, pl.ds(0, fields)], spec_sem.at[g]
        )

    small = [
        pltpu.make_async_copy(order_hbm, order_smem, small_sem.at[0]),
        pltpu.make_async_copy(pair_hbm, pair_smem, small_sem.at[1]),
        pltpu.make_async_copy(nlon_hbm, nlon_smem, small_sem.at[2]),
        pltpu.make_async_copy(gauss_hbm, gauss_smem, small_sem.at[3]),
        pltpu.make_async_copy(order_hbm, order_row.at[0], small_sem.at[4]),
    ]
    for copy in small:
        copy.start()
    for g in range(groups):
        spec_copy(g).start()
        leg_copy(g).start()

    barrier = pltpu.get_barrier_semaphore()

    def wrapped(me, step, count):
        return jnp.where(me + step >= count, me + step - count, me + step)

    def hops(step, count):
        return min(step, count - step)

    across = 4 if levels % 4 == 0 else 1
    down = levels // across
    lev_y = lev // across
    lev_x = lev % across
    cores = 2
    peers = {"wave": [], "lev": []}
    for step in range(1, waves):
        peers["wave"].append((hops(step, waves) / cores, wrapped(wave, step, waves)))
    for dy in range(down):
        for dx in range(across):
            if dy or dx:
                there = wrapped(lev_y, dy, down) * across + wrapped(lev_x, dx, across)
                peers["lev"].append((hops(dy, down) + hops(dx, across), there))
    for axis in peers:
        peers[axis].sort(key=lambda peer: -peer[0])
    greeted = [(far, axis, there) for axis in peers for far, there in peers[axis]]
    for _, axis, there in sorted(greeted, key=lambda peer: -peer[0]):
        pl.semaphore_signal(barrier, inc=1, device_id={axis: there}, device_id_type=MESH)

    def exchange(axis, me, count, source, target, index):
        for _, there in peers[axis]:
            pltpu.make_async_remote_copy(
                src_ref=source.at[there],
                dst_ref=target.at[me],
                send_sem=send_sem.at[index],
                recv_sem=recv_sem.at[index],
                device_id={axis: there},
                device_id_type=MESH,
            ).start()

        if index < 3:
            target[me] = source[me]
        else:
            pltpu.make_async_copy(source.at[me], target.at[me], out_sem.at[0]).start()

    def arrived(count, target, index):
        all_but_one = target.at[pl.ds(0, count - 1)]
        pltpu.make_async_copy(all_but_one, all_but_one, recv_sem.at[index]).wait()

    def left(count, source, index):
        all_but_one = source.at[pl.ds(0, count - 1)]
        pltpu.make_async_copy(all_but_one, all_but_one, send_sem.at[index]).wait()

    cube[...] = jnp.zeros_like(cube)
    for copy in small:
        copy.wait()
    degree = lax.broadcasted_iota(jnp.int32, (8, modes), 1)
    sign = (1 - 2 * (degree % 2)).astype(F32)

    def forward_row(r):
        order = order_smem[wave * rows + r]
        turn = (1 - 2 * (order % 2)).astype(F32)
        north = jnp.where(degree >= order, spec[r].reshape(8, modes).astype(F32), 0.0)
        south = north * sign
        both = jnp.concatenate([north, south], axis=0).astype(BF16)
        sums = nt(both, leg[r])
        cube[pl.ds(pl.multiple_of(r * 8, 8), 8), : sums.shape[1]] = sums[:8]
        cube[pl.ds(pl.multiple_of((HALF + r) * 8, 8), 8), : sums.shape[1]] = sums[8:] * turn

    per_group = group_rows // ROWS_AT_ONCE
    for g in range(groups):
        spec_copy(g).wait()
        leg_copy(g).wait()

        @pl.loop(0, per_group)
        def _(i):
            for k in range(ROWS_AT_ONCE):
                forward_row(g * group_rows + i * ROWS_AT_ONCE + k)

    picker = one_hot(pair_smem, waves)
    for c in range(8):
        if c < parts:
            block = cube[pl.ds(c, 2 * HALF, stride=8), :].astype(BF16)
            flat[pl.ds(c, waves, stride=8), :] = nt(picker, block)
        else:
            flat[pl.ds(c, waves, stride=8), :] = jnp.zeros((waves, SEG), F32)
    send_a[...] = flat[...].reshape(waves, 8, SEG).astype(BF16)

    pl.semaphore_wait(barrier, waves + levels - 2)
    exchange("wave", wave, waves, send_a, recv_a, 0)

    picker_ref[...] = picker
    for r in range(rows):
        own_ref[r : r + 1, :] = jnp.full((1, SEG), order_smem[wave * rows + r].astype(F32))
    gap = jnp.zeros((1, HALF - rows), F32)
    for j in range(chunks):
        first = order_row[:, 2 * j * rows : (2 * j + 1) * rows].astype(F32)
        second = order_row[:, (2 * j + 1) * rows : (2 * j + 2) * rows].astype(F32)
        lanes_ref[j : j + 1, :] = jnp.concatenate([first, gap, second, gap], axis=1)

    pair = pair_smem[wave]
    count = nlon_smem[pair]
    points = jnp.full((1, SEG), count.astype(F32))
    inverse = 1.0 / points
    near_k = lax.broadcasted_iota(jnp.int32, (NEAR, SEG), 0).astype(F32)
    segment = SEG * lax.broadcasted_iota(jnp.int32, (levels, SEG), 0)
    far_k = jnp.concatenate([segment + s for s in range(0, SEG, NEAR)], axis=0).astype(F32)

    @pl.loop(0, chunks)
    def _(j):
        orders = lanes_ref[pl.ds(j, 1), :]
        cosine, sine = unit_circle(near_k * orders, points, inverse)
        near_c[j] = cosine
        near_s[j] = sine
        cosine, sine = unit_circle(far_k * orders, points, inverse)
        both = jnp.concatenate([cosine, -sine], axis=1)
        high = both.astype(BF16).astype(F32)
        far[:, pl.ds(pl.multiple_of(j * 2 * SEG, SEG), 2 * SEG)] = jnp.concatenate(
            [high, both - high], axis=0
        ).astype(BF16)

    arrived(waves, recv_a, 0)

    first_half = lax.broadcasted_iota(jnp.int32, (8, SEG), 1) < HALF

    def turn_chunk(j):
        even = recv_a[2 * j].astype(F32)
        odd = recv_a[2 * j + 1].astype(F32)
        inside = jnp.where(2.0 * lanes_ref[pl.ds(j, 1), :] < points, 1.0, 0.0)
        north = jnp.where(first_half, even, pltpu.roll(odd, HALF, 1)) * inside
        south = jnp.where(first_half, pltpu.roll(even, HALF, 1), odd) * inside
        cosine = near_c[j]
        sine = near_s[j]
        first = pl.ds(j * 2 * SEG, SEG)
        second = pl.ds(j * 2 * SEG + SEG, SEG)
        for h, half in enumerate((north, south)):
            for f in range(fields):
                real = half[2 * f : 2 * f + 1]
                imag = half[2 * f + 1 : 2 * f + 2]
                place = slice((h * fields + f) * NEAR, (h * fields + f + 1) * NEAR)
                turned[place, first] = (real * cosine - imag * sine).astype(BF16)
                turned[place, second] = (real * sine + imag * cosine).astype(BF16)

    for j in range(chunks):
        turn_chunk(j)

    splits = SEG // NEAR
    quarter = lax.broadcasted_iota(jnp.int32, (levels, SEG), 1) // NEAR

    def swap(blocks):
        results = []
        for p in range(splits):
            result = blocks[p]
            for q, block in enumerate(blocks):
                if q != p:
                    moved = pltpu.roll(block, ((q - p) * NEAR) % SEG, 1)
                    result = jnp.where(quarter == q, moved, result)
            results.append(result)
        return results

    longitude = segment + lax.broadcasted_iota(jnp.int32, (levels, SEG), 1)
    scale = jnp.where(longitude < count, 1.0 / math.sqrt(modes), 0.0)
    sums = nt(turned[...], far[...])
    sums = sums[:, : splits * levels] + sums[:, splits * levels :]
    for first in range(0, parts, splits):
        held_parts = min(splits, parts - first)
        block = sums[first * NEAR : (first + held_parts) * NEAR]
        if held_parts < splits:
            block = jnp.concatenate(
                [block, jnp.zeros((SEG - block.shape[0], block.shape[1]), F32)], axis=0
            )
        block = block.T
        blocks = swap([block[q * levels : (q + 1) * levels] for q in range(splits)])
        for p in range(held_parts):
            flat_p[pl.ds(first + p, levels, stride=8), :] = blocks[p] * scale
    for c in range(parts, 8):
        flat_p[pl.ds(c, levels, stride=8), :] = jnp.zeros((levels, SEG), F32)
    send_f[...] = flat_p[...].reshape(levels, 8, SEG).astype(send_f.dtype)
    exchange("lev", lev, levels, send_f, recv_f, 1)
    arrived(levels, recv_f, 1)

    flat_p[...] = recv_f[...].astype(F32).reshape(levels * 8, SEG)
    level_row = lax.broadcasted_iota(jnp.int32, (levels, levels), 0)
    level_lane = lax.broadcasted_iota(jnp.int32, (levels, levels), 1)
    above = jnp.where(level_lane >= level_row, 1.0, 0.0)
    products = []
    for h in range(2):
        east, north, heat = (
            flat_p[pl.ds(h * fields + f, levels, stride=8), :] for f in range(fields)
        )
        for f, value in enumerate((east, north, heat)):
            grid_ref[h, f] = value
        geopotential = jnp.dot(
            above, heat, precision=lax.Precision.HIGHEST, preferred_element_type=F32
        ) * (1.0 / math.sqrt(levels))
        products += [east * heat, north * heat, east * north + geopotential]
    for hf, value in enumerate(products):
        flat_p[pl.ds(hf, levels, stride=8), :] = value
    send_p[...] = flat_p[...].reshape(levels, 8, SEG).astype(BF16)
    exchange("lev", lev, levels, send_p, recv_p, 2)
    arrived(levels, recv_p, 2)

    flat_p[...] = recv_p[...].astype(F32).reshape(levels * 8, SEG)
    for first in range(0, parts, splits):
        held_parts = min(splits, parts - first)
        blocks = [flat_p[pl.ds(first + p, levels, stride=8), :] for p in range(held_parts)]
        blocks += [jnp.zeros((levels, SEG), F32)] * (splits - held_parts)
        block = jnp.concatenate(swap(blocks), axis=0).T[: held_parts * NEAR]
        turned_p[first * NEAR : (first + held_parts) * NEAR] = jnp.concatenate(
            [block, block], axis=1
        ).astype(BF16)
    total[...] = jnp.zeros_like(total)

    root = lax.rsqrt(points)
    factors = [root * gauss_smem[2 * pair + h] for h in range(2)]

    def return_chunk(j, total):
        cosine = near_c[j]
        sine = near_s[j]
        inner = jnp.dot(
            turned_p[...],
            far[:, pl.ds(j * 2 * SEG, 2 * SEG)],
            preferred_element_type=F32,
        )
        for h in range(2):
            for f in range(fields):
                place = slice((h * fields + f) * NEAR, (h * fields + f + 1) * NEAR)
                even = inner[place, :SEG]
                odd = inner[place, SEG:]
                real = jnp.sum(even * cosine + odd * sine, axis=0, keepdims=True)
                imag = jnp.sum(odd * cosine - even * sine, axis=0, keepdims=True)
                total[h, 2 * f : 2 * f + 1] = real
                total[h, 2 * f + 1 : 2 * f + 2] = imag
        inside = jnp.where(2.0 * lanes_ref[pl.ds(j, 1), :] < points, 1.0, 0.0)
        north = total[0] * (factors[0] * inside)
        south = total[1] * (factors[1] * inside)
        send_d[2 * j] = jnp.where(first_half, north, pltpu.roll(south, HALF, 1)).astype(BF16)
        send_d[2 * j + 1] = jnp.where(first_half, pltpu.roll(north, HALF, 1), south).astype(BF16)

    for j in range(chunks):
        return_chunk(j, total.at[j])

    exchange("wave", wave, waves, send_d, recv_d, 3)
    arrived(waves, recv_d, 3)

    pltpu.make_async_copy(send_d.at[wave], recv_d.at[wave], out_sem.at[0]).wait()

    for index, (size, source) in enumerate(
        ((waves, send_a), (levels, send_f), (levels, send_p), (waves, send_d))
    ):
        left(size, source, index)


def back_kernel(
    waves, fields, rows, modes,
    recv, picker_ref, own_ref, grid, leg,
    grid_hbm, tend_hbm,
    tend, flat, cube, out_sem,
):
    parts = 2 * fields
    groups = out_sem.shape[0] - 1
    group_rows = rows // groups

    def tend_copy(g):
        block = pl.ds(g * group_rows, group_rows)
        return pltpu.make_async_copy(
            tend.at[block, pl.ds(0, fields)], tend_hbm.at[block], out_sem.at[g]
        )

    grid_copy = pltpu.make_async_copy(grid, grid_hbm, out_sem.at[groups])
    grid_copy.start()
    degree = lax.broadcasted_iota(jnp.int32, (8, modes), 1)
    sign = (1 - 2 * (degree % 2)).astype(F32)
    place = degree.astype(F32)
    outer = math.sqrt(modes / (2 * waves))
    picker = picker_ref[...]
    flat[...] = recv[...].astype(F32).reshape(waves * 8, SEG)
    for c in range(parts):
        block = flat[pl.ds(c, waves, stride=8), :].astype(BF16)
        cube[pl.ds(c, 2 * HALF, stride=8), :] = lax.dot_general(
            block, picker, (((0,), (0,)), ((), ())), preferred_element_type=F32
        )
    for c in range(parts, 8):
        cube[pl.ds(c, 2 * HALF, stride=8), :] = jnp.zeros((2 * HALF, SEG), F32)

    def backward_row(r):
        order = own_ref[pl.ds(r, 1), :1]
        turn = 1.0 - 2.0 * (order - 2.0 * jnp.floor(0.5 * order))
        north = cube[pl.ds(pl.multiple_of(r * 8, 8), 8), :]
        south = cube[pl.ds(pl.multiple_of((HALF + r) * 8, 8), 8), :] * turn
        both = jnp.concatenate([north, south], axis=0)[:, :waves].astype(BF16)
        sums = jnp.dot(both, leg[r], preferred_element_type=F32)
        mixed = (sums[:8] + sums[8:] * sign) * outer
        mixed = jnp.where(place >= order, mixed, 0.0).astype(BF16)
        tend[r] = mixed.reshape(4, 2, modes)

    for g in range(groups):

        @pl.loop(0, group_rows // ROWS_AT_ONCE)
        def _(i):
            for k in range(ROWS_AT_ONCE):
                backward_row(g * group_rows + i * ROWS_AT_ONCE + k)

        tend_copy(g).start()

    for g in range(groups):
        tend_copy(g).wait()
    grid_copy.wait()


def local(spectral, legendre, gauss, wave_order, pair_order, nlon):
    rows, _, fields, _, modes = spectral.shape
    waves = lax.axis_size("wave")
    levels = lax.axis_size("lev")
    parts = 2 * fields
    spec = jnp.transpose(spectral, (0, 2, 3, 1, 4)).reshape(rows, fields, 2, modes)
    anywhere = pl.BlockSpec(memory_space=pl.ANY)
    groups = max(g for g in (1, 2, 3, 6) if rows % (g * ROWS_AT_ONCE) == 0)
    chunks = waves // 2
    scratch = [
        pltpu.SMEM(wave_order.shape, jnp.int32),
        pltpu.SMEM(pair_order.shape, jnp.int32),
        pltpu.SMEM(nlon.shape, jnp.int32),
        pltpu.SMEM(gauss.shape, F32),
        pltpu.VMEM((1, *wave_order.shape), jnp.int32),
        pltpu.VMEM((chunks, SEG), F32),
        pltpu.VMEM((rows, 4, 2, modes), BF16),
        pltpu.VMEM((2 * HALF * 8, SEG), F32),
        pltpu.VMEM((waves * 8, SEG), F32),
        pltpu.VMEM((waves, 8, SEG), BF16),
        pltpu.VMEM((waves, 8, SEG), BF16),
        pltpu.VMEM((chunks, NEAR, SEG), F32),
        pltpu.VMEM((chunks, NEAR, SEG), F32),
        pltpu.VMEM((2 * levels * SEG // NEAR, chunks * 2 * SEG), BF16),
        pltpu.VMEM((parts * NEAR, chunks * 2 * SEG), BF16),
        pltpu.VMEM((levels, 8, SEG), BF16),
        pltpu.VMEM((levels, 8, SEG), BF16),
        pltpu.VMEM((levels * 8, SEG), F32),
        pltpu.VMEM((levels, 8, SEG), BF16),
        pltpu.VMEM((levels, 8, SEG), BF16),
        pltpu.VMEM((parts * NEAR, 2 * levels * SEG // NEAR), BF16),
        pltpu.VMEM((chunks, 2, 8, SEG), F32),
        pltpu.VMEM((waves, 8, SEG), BF16),
        pltpu.SemaphoreType.DMA((5,)),
        pltpu.SemaphoreType.DMA((groups,)),
        pltpu.SemaphoreType.DMA((groups,)),
        pltpu.SemaphoreType.DMA((1,)),
        pltpu.SemaphoreType.DMA((4,)),
        pltpu.SemaphoreType.DMA((4,)),
    ]
    inputs = (wave_order, pair_order, nlon, gauss, spec, legendre)
    grid_shape = jax.ShapeDtypeStruct((2, fields, levels, SEG), F32)
    far_memory = pl.BlockSpec(memory_space=pltpu.HBM)
    vmem = pl.BlockSpec(memory_space=pltpu.VMEM)
    grid, weighted, picker, own, table = pl.pallas_call(
        functools.partial(kernel, waves, levels, fields, rows, modes),
        out_shape=(
            grid_shape,
            jax.ShapeDtypeStruct((waves, 8, SEG), BF16),
            jax.ShapeDtypeStruct((waves, SEG), BF16),
            jax.ShapeDtypeStruct((rows, SEG), F32),
            jax.ShapeDtypeStruct(legendre.shape, BF16),
        ),
        in_specs=[far_memory] * 6,
        out_specs=(vmem, anywhere, vmem, vmem, vmem),
        scratch_shapes=scratch,
        compiler_params=pltpu.CompilerParams(
            collective_id=0, has_side_effects=True, vmem_limit_bytes=VMEM_LIMIT
        ),
    )(*(pltpu.with_memory_space_constraint(x, pltpu.HBM) for x in inputs))
    grid, tend = pl.pallas_call(
        functools.partial(back_kernel, waves, fields, rows, modes),
        out_shape=(grid_shape, jax.ShapeDtypeStruct(spec.shape, BF16)),
        in_specs=[vmem] * 5,
        out_specs=(anywhere, anywhere),
        scratch_shapes=[
            pltpu.VMEM((rows, 4, 2, modes), BF16),
            pltpu.VMEM((waves * 8, SEG), F32),
            pltpu.VMEM((2 * HALF * 8, SEG), F32),
            pltpu.SemaphoreType.DMA((groups + 1,)),
        ],
        compiler_params=pltpu.CompilerParams(vmem_limit_bytes=VMEM_LIMIT),
    )(weighted, picker, own, grid, table)
    tend = tend.reshape(rows, fields, 1, 2, modes)
    return grid, jnp.transpose(tend, (0, 3, 1, 2, 4))


def solution(mesh):
    in_specs = (P("wave", None, None, "lev", None), P("wave", None, None), P(), P(), P(), P())
    out_specs = (P("wave", None, None, "lev"), P("wave", None, None, "lev", None))
    return jax.shard_map(local, mesh=mesh, in_specs=in_specs, out_specs=out_specs, check_vma=False)
```
